32 devices in a mesh: patch: 16 (over z, y, x), frame: 2 (over core).
Axes of the slice: x: 2, y: 2, z: 4, core: 2. Of those that a mesh axis runs over, the one named last changes fastest.
Arguments:
- basis: bfloat16 [3, 4096, 1024], P(None, 'patch'), may hold values from -0.25 to 0.25
- latents: bfloat16 [1024, 1024], P('frame', 'patch'), may hold values from -2 to 2
- rest_pos: float32 [3, 4096], P(None, 'patch'), may hold values from -3 to 3
- triangles: int32 [3, 8192], P(None, 'patch'), may hold values from 0 to 511
- hinges: int32 [4, 6144], P(None, 'patch'), may hold values from 0 to 511
- rest_sq: float32 [3, 8192], P(None, 'patch'), may hold values from 0.5 to 3
- bend_rest: float32 [3, 6144], P(None, 'patch'), may hold values from -5 to 5
- masses: float32 [4096], P('patch'), may hold values from 0.5 to 2
- send_rows: int32 [2, 2048], P(None, 'patch'), may hold values from 0 to 255, as said below
Outputs:
- basis_grad: float32 [3, 4096, 1024], P(None, ('patch', 'frame'))
- latent_grad: float32 [1024, 1024], P('frame', 'patch')
The draws below stay inside these ranges and needn't reach their ends.
Inputs may be any that keep to these rules, and one draw needn't show every extreme that they name: `send_rows`: within one patch's columns the 256 entries of both rows are distinct own vertex numbers.
All inputs are finite; a program needn't handle non-finite values.
Results may differ from the reference program's by a relative error of at most 0.006.
Values may be sent and summed in bfloat16 or wider, within the bound.
A program may use at most 64 MiB of HBM per device.

```python
import math
import jax
import jax.numpy as jnp
from jax import lax

LATENT = 1024
VDEV = 256
FR_DEV = 512
HALO = 128
VERTS = 4096
FRAMES = 1024
TRIS = 8192
HINGES = 6144
N_PATCH = 16
N_FRAME = 2


def draw_send_rows(key, part):
    keys = jax.random.split(jax.random.fold_in(key, 17), N_PATCH)

    def one_patch(patch_key):
        shuffled = jax.random.permutation(patch_key, VDEV)
        return shuffled[:2 * HALO].reshape(2, HALO)
    chosen = jax.vmap(one_patch)(keys)
    return jnp.transpose(chosen, (1, 0, 2)).reshape(2, N_PATCH * HALO).astype(jnp.int32)


def plant(values, rng, low, high):
    longest = values.shape.index(max(values.shape))
    spots = []
    for shift in (0, 1):
        where = [jax.random.randint(jax.random.fold_in(rng, axis), (), 0, length) for axis, length in enumerate(values.shape)]
        where[longest] = (where[longest] + shift) % values.shape[longest]
        spots.append(tuple(where))
    return values.at[spots[0]].set(low).at[spots[1]].set(high)


def spiked(entries, own_key, source, target, shards_of, factor):
    def block_of(position):
        return (jnp.arange(entries.shape[position]) // (entries.shape[position] // shards_of)).reshape((-1,) + (1,) * (entries.ndim - 1 - position))

    one_side = jax.random.permutation(own_key, shards_of)[block_of(target)]
    second = (block_of(target) + shards_of // 2) % shards_of
    return jnp.where((block_of(source) == one_side) | (block_of(source) == second), factor * entries, entries)


def shard_levels(key, dims, pieces, least, largest):
    loudness, own = 1.0, jax.random.fold_in(key, 6)
    for axis_at, blocks in pieces:
        steps = jnp.exp(jax.random.uniform(jax.random.fold_in(own, axis_at), (blocks,), jnp.float32, least / len(pieces), largest / len(pieces)))
        loudness = loudness * jnp.repeat(steps, dims[axis_at] // blocks).reshape([-1 if axis == axis_at else 1 for axis in range(len(dims))])
    return loudness


def centred(key, extent, width, most, cuts=(), held_as=jnp.bfloat16):
    result = jax.random.normal(key, extent, jnp.float32) * width
    if len(cuts) > 0:
        result = shard_levels(key, extent, cuts, -0.22, 0.18) * result
    return jnp.clip(result, min=-most, max=most).astype(held_as)


def heavy_noise(key, extent, deviation, reach, cuts, heavy, kind=jnp.bfloat16):
    values = deviation * jax.random.normal(key, extent, jnp.float32)
    if cuts:
        values = values * shard_levels(key, extent, cuts, -0.22, 0.18)
    return jnp.clip(spiked(values, jax.random.fold_in(key, 3), *heavy), -reach, reach).astype(kind)


def setup_inputs(seed: int = 0) -> dict:
    splits = jax.random.split(jax.random.key(seed), 10)
    basis = heavy_noise(splits[0], (3, VERTS, LATENT), LATENT ** -0.5, 0.25, ((1, 16),), (1, 2, 16, 2.0))
    latents = centred(splits[1], (FRAMES, LATENT), 0.3, 2.0, ((0, 2), (1, 16)))
    rest_pos = centred(splits[2], (3, VERTS), 0.5, 3.0, ((1, 16),), jnp.float32)
    triangles = plant(jax.random.randint(splits[3], (3, TRIS), 0, VDEV + 2 * HALO), jax.random.fold_in(splits[3], 1), 0, (VDEV + 2 * HALO) - 1).astype(jnp.int32)
    hinges = plant(jax.random.randint(splits[4], (4, HINGES), 0, VDEV + 2 * HALO), jax.random.fold_in(splits[4], 1), 0, (VDEV + 2 * HALO) - 1).astype(jnp.int32)
    rest_sq = jnp.clip(jnp.exp(math.log(3.0) - 1.7917595 * jax.random.uniform(splits[5], (3, TRIS), jnp.float32) ** shard_levels(splits[5], (3, TRIS), ((1, 16),), -0.2, 0.2)), 0.5, 3.0)
    bend_rest = centred(splits[6], (3, HINGES), 1.0, 5.0, ((1, 16),), jnp.float32)
    masses = jnp.clip(jnp.exp(math.log(2.0) - 1.3862944 * jax.random.uniform(splits[7], (VERTS,), jnp.float32) ** shard_levels(splits[7], (VERTS,), ((0, 16),), -0.2, 0.2)), 0.5, 2.0)
    send_rows = draw_send_rows(jax.random.fold_in(splits[9], 71), 0)
    return dict(basis=basis, latents=latents, rest_pos=rest_pos, triangles=triangles, hinges=hinges, rest_sq=rest_sq, bend_rest=bend_rest, masses=masses, send_rows=send_rows)


MEMBRANE = 5.0
BENDING = 5.0
GRAVITY = 40.0

def elastic(points, corners, hinge_ids, rest_sq, bend_rest):
    point_one = points[:, :, corners[0]]
    point_two = points[:, :, corners[1]]
    point_three = points[:, :, corners[2]]
    edge_list = (point_two - point_one, point_three - point_two, point_one - point_three)
    membrane = jnp.float32(0.0)
    for corner_slot in range(3):
        strain = lax.optimization_barrier(jnp.sum(edge_list[corner_slot] * edge_list[corner_slot], axis=1)) - rest_sq[corner_slot]
        membrane = membrane + jnp.sum(strain * strain)
    bending = points[:, :, hinge_ids[2]] + points[:, :, hinge_ids[3]] - points[:, :, hinge_ids[0]] - points[:, :, hinge_ids[1]] - bend_rest
    return MEMBRANE * membrane + BENDING * jnp.sum(bending * bending)

def extend_ids(local_ids, send_rows):
    row_count = local_ids.shape[0]
    grouped = local_ids.reshape(row_count, N_PATCH, -1)
    senders = send_rows.reshape(2, N_PATCH, HALO)
    device_ids = jnp.arange(N_PATCH, dtype=jnp.int32)[None, :, None]
    previous = (device_ids + N_PATCH - 1) % N_PATCH
    following = (device_ids + 1) % N_PATCH
    from_prev = senders[1][previous, jnp.clip(grouped - VDEV, 0, HALO - 1)] + previous * VDEV
    from_next = senders[0][following, jnp.clip(grouped - VDEV - HALO, 0, HALO - 1)] + following * VDEV
    global_ids = jnp.where(grouped < VDEV, grouped + device_ids * VDEV, jnp.where(grouped < VDEV + HALO, from_prev, from_next))
    return global_ids.reshape(row_count, -1).astype(jnp.int32)

def reference(basis, latents, rest_pos, triangles, hinges, rest_sq, bend_rest, masses, send_rows):
    corners = extend_ids(triangles, send_rows)
    hinge_ids = extend_ids(hinges, send_rows)
    flat_basis = basis.reshape(3 * VERTS, LATENT)
    decoded = jnp.dot(latents, flat_basis.T, preferred_element_type=jnp.float32)
    positions = rest_pos[None] + decoded.reshape(FRAMES, 3, VERTS)
    frame_block = min(32, FRAMES)
    stacked = positions.reshape(FRAMES // frame_block, frame_block, 3, VERTS)
    force_fn = jax.grad(elastic)
    grads = lax.map(lambda frames_block: force_fn(frames_block, corners, hinge_ids, rest_sq, bend_rest), stacked)
    grads = grads.reshape(FRAMES, 3, VERTS)
    grads = grads.at[:, 2, :].add(GRAVITY * masses)
    adjoint = (grads / FRAMES).astype(jnp.bfloat16)
    flat_adjoint = adjoint.reshape(FRAMES, 3 * VERTS)
    latent_grad = jnp.dot(flat_adjoint, flat_basis, preferred_element_type=jnp.float32)
    total = jnp.zeros((3 * VERTS, LATENT), jnp.float32)
    for half_index in range(N_FRAME):
        lower = half_index * FR_DEV
        partial_sum = jnp.dot(flat_adjoint[lower:lower + FR_DEV].T, latents[lower:lower + FR_DEV], preferred_element_type=jnp.float32)
        rounded = lax.optimization_barrier(partial_sum.astype(jnp.bfloat16))
        total = total + rounded.astype(jnp.float32)
    return (total.reshape(3, VERTS, LATENT), latent_grad)
```

```python
import jax
import jax.numpy as jnp
from jax import lax
from jax.sharding import PartitionSpec as P

MEMBRANE = 5.0
BENDING = 5.0
GRAVITY = 40.0
BF = jnp.bfloat16
F32 = jnp.float32


def shift(block, step):
    n = lax.axis_size("patch")
    return lax.ppermute(block, "patch", [(i, (i + step) % n) for i in range(n)])


def hot(rows, ids):
    iota = lax.broadcasted_iota(jnp.int32, (rows, ids.shape[0]), 0)
    return (iota == ids[None, :]).astype(F32)


def mm(a, b, dims):
    return lax.dot_general(a, b, (dims, ((), ())), preferred_element_type=F32)


def exact(a, b):
    return jnp.dot(a, b, precision=lax.Precision.HIGHEST, preferred_element_type=F32)


def local(basis, latents, rest_pos, triangles, hinges, rest_sq, bend_rest, masses, send_rows):
    vs = basis.shape[1]
    kk = basis.shape[2]
    ff = latents.shape[0]
    halo = send_rows.shape[1]
    nt = triangles.shape[1]
    total = ff * lax.axis_size("frame")
    pos = lax.axis_index("frame")
    lat_t = lax.all_gather(latents.T, "patch", axis=0, tiled=True)
    lat_o = lax.ppermute(lat_t, "frame", [(0, 1), (1, 0)])
    ext = vs + 2 * halo
    ta, tb, tc = (hot(ext, triangles[i]) for i in range(3))
    ha, hb, hc, hd = (hot(ext, hinges[i]) for i in range(4))
    inc = jnp.concatenate([tb - ta, tc - tb, hc + hd - ha - hb], axis=1).astype(BF)
    self32 = hot(vs, send_rows.reshape(-1))
    sel = self32.astype(BF)
    rest_out = exact(rest_pos, self32)
    rest_ext = jnp.concatenate(
        [rest_pos, shift(rest_out[:, halo:], 1), shift(rest_out[:, :halo], -1)], axis=1
    )
    rest_edge = exact(rest_ext, inc.astype(F32))
    rest_edge = rest_edge.at[:, 2 * nt :].add(-bend_rest)
    flat_basis = basis.reshape(3 * vs, kk)
    dec = mm(flat_basis, lat_t, ((1,), (0,))).astype(BF).reshape(3, vs, ff)
    own = jnp.concatenate([dec[0], dec[1], dec[2]], axis=1)
    out = mm(sel, own, ((0,), (0,))).astype(BF)
    dext = jnp.concatenate([own, shift(out[halo:], 1), shift(out[:halo], -1)], axis=0)
    edges = mm(inc, dext, ((0,), (0,)))
    e1 = [edges[:nt, c * ff : (c + 1) * ff] + rest_edge[c, :nt, None] for c in range(3)]
    e2 = [edges[nt : 2 * nt, c * ff : (c + 1) * ff] + rest_edge[c, nt : 2 * nt, None] for c in range(3)]
    hh = [edges[2 * nt :, c * ff : (c + 1) * ff] + rest_edge[c, 2 * nt :, None] for c in range(3)]
    e3 = [-(a + b) for a, b in zip(e1, e2)]
    k = 4.0 * MEMBRANE / total

    def strain(e, r):
        return k * (e[0] * e[0] + e[1] * e[1] + e[2] * e[2] - r[:, None])

    s1, s2, s3 = strain(e1, rest_sq[0]), strain(e2, rest_sq[1]), strain(e3, rest_sq[2])
    u1 = jnp.concatenate([s1 * e1[c] - s3 * e3[c] for c in range(3)], axis=1)
    u2 = jnp.concatenate([s2 * e2[c] - s3 * e3[c] for c in range(3)], axis=1)
    uh = jnp.concatenate(hh, axis=1) * (2.0 * BENDING / total)
    forces = jnp.concatenate([u1, u2, uh], axis=0).astype(BF)
    g = mm(inc, forces, ((1,), (0,)))
    gh = g[vs:].astype(BF)
    back = jnp.concatenate([shift(gh[halo:], 1), shift(gh[:halo], -1)], axis=0)
    owned = g[:vs] + mm(sel, back, ((1,), (0,)))
    owned = owned.at[:, 2 * ff :].add((GRAVITY / total) * masses[:, None])
    adj = owned.astype(BF)
    half = vs // 2
    mine = lax.dynamic_slice_in_dim(adj, pos * half, half, 0)
    other = lax.dynamic_slice_in_dim(adj, (1 - pos) * half, half, 0)
    got = lax.ppermute(other, "frame", [(0, 1), (1, 0)])

    def part(a, lat):
        a3 = jnp.concatenate([a[:, c * ff : (c + 1) * ff] for c in range(3)], axis=0)
        s = lax.optimization_barrier(mm(a3, lat, ((1,), (1,))).astype(BF))
        return s.astype(F32).reshape(3, half, kk)

    basis_grad = part(mine, lat_t) + part(got, lat_o)
    adj3 = jnp.concatenate([adj[:, c * ff : (c + 1) * ff] for c in range(3)], axis=0)
    lg_t = mm(flat_basis, adj3, ((0,), (0,)))
    lg = lax.psum_scatter(lg_t, "patch", scatter_dimension=0, tiled=True)
    return (basis_grad, lg.T)


def solution(mesh):
    return jax.shard_map(
        local,
        mesh=mesh,
        in_specs=(
            P(None, "patch", None),
            P("frame", "patch"),
            P(None, "patch"),
            P(None, "patch"),
            P(None, "patch"),
            P(None, "patch"),
            P(None, "patch"),
            P("patch"),
            P(None, "patch"),
        ),
        out_specs=(P(None, ("patch", "frame"), None), P("frame", "patch")),
        check_vma=False,
    )
```

```python
import functools

import jax
import jax.numpy as jnp
from jax import lax
from jax.experimental import pallas as pl
from jax.experimental.pallas import tpu as pltpu
from jax.sharding import PartitionSpec as P

MEMBRANE = 5.0
BENDING = 5.0
GRAVITY = 40.0
BF = jnp.bfloat16
F32 = jnp.float32


def shift(block, step):
    n = lax.axis_size("patch")
    return lax.ppermute(block, "patch", [(i, (i + step) % n) for i in range(n)])


def hot(rows, ids):
    iota = lax.broadcasted_iota(jnp.int32, (rows, ids.shape[0]), 0)
    return (iota == ids[None, :]).astype(F32)


def mm(a, b, dims):
    return lax.dot_general(a, b, (dims, ((), ())), preferred_element_type=F32)


def exact(a, b):
    return jnp.dot(a, b, precision=lax.Precision.HIGHEST, preferred_element_type=F32)


PLANE = 4
MESH_ID = pl.DeviceIdType.MESH
DMA = pltpu.SemaphoreType.DMA


def places(n):
    p = lax.axis_index("patch")
    xnb = p + 1 - 2 * (p % 2)
    ynb = p + 2 - 4 * ((p // 2) % 2)
    return p, p // PLANE, p % PLANE, xnb, ynb


def greet(peers):
    bar = pltpu.get_barrier_semaphore()
    for q in peers:
        pl.semaphore_signal(bar, inc=1, device_id={"patch": q}, device_id_type=MESH_ID)
    pl.semaphore_wait(bar, len(peers))


def send(src, dst, ss, rs, q):
    return pltpu.make_async_remote_copy(
        src_ref=src, dst_ref=dst, send_sem=ss, recv_sem=rs,
        device_id={"patch": q}, device_id_type=MESH_ID,
    )


def gather_kernel(n, w, x_ref, o_ref, zs, zr, xs, xr, ys, yr, rs, rr):
    hi = n // PLANE
    p, h, lo, xnb, ynb = places(n)
    lox, loy = xnb % PLANE, ynb % PLANE

    def rows(hh, ll):
        return o_ref.at[pl.ds(pl.multiple_of((hh * PLANE + ll) * w, w), w)]

    zpeer = [((h + j) % hi) * PLANE + lo for j in range(hi)]
    greet(zpeer[1:] + [xnb, ynb])
    order = sorted(range(1, hi), key=lambda j: min(j, hi - j))
    mine = rows(h, lo)
    zc = {j: send(x_ref, mine, zs.at[j], zr.at[j], zpeer[j]) for j in order}
    xc, yc, rc = {}, {}, {}
    xc[0] = send(x_ref, mine, xs.at[0], xr.at[0], xnb)
    yc[0] = send(x_ref, mine, ys.at[0], yr.at[0], ynb)
    xc[0].start()
    yc[0].start()
    for j in reversed(order):
        zc[j].start()
    mine[...] = x_ref[...]

    def relay(j):
        hh = (h + hi - j) % hi
        if j % 2 == 0:
            xc[j].wait_recv()
            part = rows(hh, lox)
            rc[j] = send(part, part, rs.at[j], rr.at[j], ynb)
        else:
            yc[j].wait_recv()
            part = rows(hh, loy)
            rc[j] = send(part, part, rs.at[j], rr.at[j], xnb)
        rc[j].start()

    last = 0
    for j in order:
        zc[j].wait_recv()
        part = rows((h + hi - j) % hi, lo)
        xc[j] = send(part, part, xs.at[j], xr.at[j], xnb)
        yc[j] = send(part, part, ys.at[j], yr.at[j], ynb)
        xc[j].start()
        yc[j].start()
        relay(last)
        last = j
    relay(last)
    for j in range(hi):
        if j % 2 == 0:
            yc[j].wait_recv()
        else:
            xc[j].wait_recv()
        rc[j].wait_recv()
    for j in range(hi):
        if j:
            zc[j].wait_send()
        xc[j].wait_send()
        yc[j].wait_send()
        rc[j].wait_send()


def gather_all(x, n):
    w, f = x.shape
    hi = n // PLANE
    return pl.pallas_call(
        functools.partial(gather_kernel, n, w),
        out_shape=jax.ShapeDtypeStruct((n * w, f), x.dtype),
        in_specs=[pl.BlockSpec(memory_space=pltpu.VMEM)],
        out_specs=pl.BlockSpec(memory_space=pltpu.VMEM),
        scratch_shapes=[DMA((hi,))] * 8,
        compiler_params=pltpu.CompilerParams(collective_id=0, has_side_effects=True),
    )(x)


def scatter_kernel(
    n, w, g_ref, o_ref, rl, sb, cx, cy, zb, zl, ls, lr, xs, xr, ys, yr, zs, zr
):
    hi = n // PLANE
    p, h, lo, xnb, ynb = places(n)
    lox, loy = xnb % PLANE, ynb % PLANE
    lod = PLANE - 1 - lo

    def rows(j, ll):
        hh = (h + j) % hi
        return g_ref.at[pl.ds(pl.multiple_of((hh * PLANE + ll) * w, w), w)]

    zpeer = [((h + j) % hi) * PLANE + lo for j in range(hi)]
    greet(zpeer[1:] + [xnb, ynb])
    order = sorted(range(1, hi), key=lambda j: -min(j, hi - j)) + [0]
    lc, xc, yc, zc = {}, {}, {}, {}
    for j in order:
        lc[j] = send(rows(j, lod), rl.at[j], ls.at[j], lr.at[j], xnb if j % 2 == 0 else ynb)
        lc[j].start()
    for j in order:
        if j % 2 == 0:
            xc[j] = send(rows(j, lox), cx.at[j], xs.at[j], xr.at[j], xnb)
            xc[j].start()
        else:
            yc[j] = send(rows(j, loy), cy.at[j], ys.at[j], yr.at[j], ynb)
            yc[j].start()
    for j in order:
        lc[j].wait_recv()
        own = rows(j, loy if j % 2 == 0 else lox)
        sb[j] = (own[...].astype(F32) + rl[j].astype(F32)).astype(BF)
        if j % 2 == 0:
            yc[j] = send(sb.at[j], cy.at[j], ys.at[j], yr.at[j], ynb)
            yc[j].start()
        else:
            xc[j] = send(sb.at[j], cx.at[j], xs.at[j], xr.at[j], xnb)
            xc[j].start()
    for j in order:
        xc[j].wait_recv()
        yc[j].wait_recv()
        s = rows(j, lo)[...].astype(F32) + cx[j].astype(F32) + cy[j].astype(F32)
        if j:
            zb[j] = s.astype(BF)
            zc[j] = send(zb.at[j], zl.at[j], zs.at[j], zr.at[j], zpeer[j])
            zc[j].start()
    for j in reversed(order[:-1]):
        zc[j].wait_recv()
        s = s + zl[j].astype(F32)
    o_ref[...] = s
    for j in order:
        lc[j].wait_send()
        xc[j].wait_send()
        yc[j].wait_send()
        if j:
            zc[j].wait_send()


def scatter_sum(g, n):
    f = g.shape[1]
    w = g.shape[0] // n
    hi = n // PLANE
    return pl.pallas_call(
        functools.partial(scatter_kernel, n, w),
        out_shape=jax.ShapeDtypeStruct((w, f), F32),
        in_specs=[pl.BlockSpec(memory_space=pltpu.VMEM)],
        out_specs=pl.BlockSpec(memory_space=pltpu.VMEM),
        scratch_shapes=[pltpu.VMEM((hi, w, f), BF)] * 6 + [DMA((hi,))] * 8,
        compiler_params=pltpu.CompilerParams(collective_id=1, has_side_effects=True),
    )(g)


def local(basis, latents, rest_pos, triangles, hinges, rest_sq, bend_rest, masses, send_rows):
    vs = basis.shape[1]
    kk = basis.shape[2]
    ff = latents.shape[0]
    halo = send_rows.shape[1]
    nt = triangles.shape[1]
    total = ff * lax.axis_size("frame")
    pos = lax.axis_index("frame")
    n = lax.axis_size("patch")
    lat_t = gather_all(latents.T, n)
    lat_o = lax.ppermute(lat_t, "frame", [(0, 1), (1, 0)])
    ext = vs + 2 * halo
    ta, tb, tc = (hot(ext, triangles[i]) for i in range(3))
    ha, hb, hc, hd = (hot(ext, hinges[i]) for i in range(4))
    inc = jnp.concatenate([tb - ta, tc - tb, hc + hd - ha - hb], axis=1).astype(BF)
    self32 = hot(vs, send_rows.reshape(-1))
    sel = self32.astype(BF)
    rest_out = exact(rest_pos, self32)
    rest_ext = jnp.concatenate(
        [rest_pos, shift(rest_out[:, halo:], 1), shift(rest_out[:, :halo], -1)], axis=1
    )
    rest_edge = exact(rest_ext, inc.astype(F32))
    rest_edge = rest_edge.at[:, 2 * nt :].add(-bend_rest)
    flat_basis = basis.reshape(3 * vs, kk)
    dec = mm(flat_basis, lat_t, ((1,), (0,))).astype(BF).reshape(3, vs, ff)
    own = jnp.concatenate([dec[0], dec[1], dec[2]], axis=1)
    out = mm(sel, own, ((0,), (0,))).astype(BF)
    dext = jnp.concatenate([own, shift(out[halo:], 1), shift(out[:halo], -1)], axis=0)
    edges = mm(inc, dext, ((0,), (0,)))
    e1 = [edges[:nt, c * ff : (c + 1) * ff] + rest_edge[c, :nt, None] for c in range(3)]
    e2 = [edges[nt : 2 * nt, c * ff : (c + 1) * ff] + rest_edge[c, nt : 2 * nt, None] for c in range(3)]
    hh = [edges[2 * nt :, c * ff : (c + 1) * ff] + rest_edge[c, 2 * nt :, None] for c in range(3)]
    e3 = [-(a + b) for a, b in zip(e1, e2)]
    k = 4.0 * MEMBRANE / total

    def strain(e, r):
        return k * (e[0] * e[0] + e[1] * e[1] + e[2] * e[2] - r[:, None])

    s1, s2, s3 = strain(e1, rest_sq[0]), strain(e2, rest_sq[1]), strain(e3, rest_sq[2])
    u1 = jnp.concatenate([s1 * e1[c] - s3 * e3[c] for c in range(3)], axis=1)
    u2 = jnp.concatenate([s2 * e2[c] - s3 * e3[c] for c in range(3)], axis=1)
    uh = jnp.concatenate(hh, axis=1) * (2.0 * BENDING / total)
    forces = jnp.concatenate([u1, u2, uh], axis=0).astype(BF)
    g = mm(inc, forces, ((1,), (0,)))
    gh = g[vs:].astype(BF)
    back = jnp.concatenate([shift(gh[halo:], 1), shift(gh[:halo], -1)], axis=0)
    owned = g[:vs] + mm(sel, back, ((1,), (0,)))
    owned = owned.at[:, 2 * ff :].add((GRAVITY / total) * masses[:, None])
    adj = owned.astype(BF)
    half = vs // 2
    mine = lax.dynamic_slice_in_dim(adj, pos * half, half, 0)
    other = lax.dynamic_slice_in_dim(adj, (1 - pos) * half, half, 0)
    got = lax.ppermute(other, "frame", [(0, 1), (1, 0)])

    def part(a, lat):
        a3 = jnp.concatenate([a[:, c * ff : (c + 1) * ff] for c in range(3)], axis=0)
        s = lax.optimization_barrier(mm(a3, lat, ((1,), (1,))).astype(BF))
        return s.astype(F32).reshape(3, half, kk)

    basis_grad = part(mine, lat_t) + part(got, lat_o)
    adj3 = jnp.concatenate([adj[:, c * ff : (c + 1) * ff] for c in range(3)], axis=0)
    lg_t = mm(flat_basis, adj3, ((0,), (0,))).astype(BF)
    lg = scatter_sum(lg_t, n)
    return (basis_grad, lg.T)


def solution(mesh):
    return jax.shard_map(
        local,
        mesh=mesh,
        in_specs=(
            P(None, "patch", None),
            P("frame", "patch"),
            P(None, "patch"),
            P(None, "patch"),
            P(None, "patch"),
            P(None, "patch"),
            P(None, "patch"),
            P("patch"),
            P(None, "patch"),
        ),
        out_specs=(P(None, ("patch", "frame"), None), P("frame", "patch")),
        check_vma=False,
    )
```

```python
import functools

import jax
import jax.numpy as jnp
from jax import lax
from jax.experimental import pallas as pl
from jax.experimental.pallas import tpu as pltpu
from jax.sharding import PartitionSpec as P

MEMBRANE = 5.0
BENDING = 5.0
GRAVITY = 40.0
BF = jnp.bfloat16
F32 = jnp.float32


def shift(block, step):
    n = lax.axis_size("patch")
    return lax.ppermute(block, "patch", [(i, (i + step) % n) for i in range(n)])


def hot(rows, ids):
    iota = lax.broadcasted_iota(jnp.int32, (rows, ids.shape[0]), 0)
    return (iota == ids[None, :]).astype(F32)


def mm(a, b, dims):
    return lax.dot_general(a, b, (dims, ((), ())), preferred_element_type=F32)


def exact(a, b):
    return jnp.dot(a, b, precision=lax.Precision.HIGHEST, preferred_element_type=F32)


PLANE = 4
MESH_ID = pl.DeviceIdType.MESH
DMA = pltpu.SemaphoreType.DMA


def places(n):
    p = lax.axis_index("patch")
    xnb = p + 1 - 2 * (p % 2)
    ynb = p + 2 - 4 * ((p // 2) % 2)
    return p, p // PLANE, p % PLANE, xnb, ynb


def greet(peers, pos=None):
    bar = pltpu.get_barrier_semaphore()
    if pos is not None:
        pl.semaphore_signal(bar, inc=1, device_id={"frame": 1 - pos}, device_id_type=MESH_ID)
    for q in peers:
        pl.semaphore_signal(bar, inc=1, device_id={"patch": q}, device_id_type=MESH_ID)
    pl.semaphore_wait(bar, len(peers) + (pos is not None))


def send(src, dst, ss, rs, q):
    return pltpu.make_async_remote_copy(
        src_ref=src, dst_ref=dst, send_sem=ss, recv_sem=rs,
        device_id={"patch": q}, device_id_type=MESH_ID,
    )


def gather_kernel(
    n, w, hs, x_ref, b0, b1, b2, r_ref, o_ref, e0, e1, e2, t_ref,
    zs, zr, xs, xr, ys, yr, rs, rr, hds, hdr, fs, fr, qs, qr
):
    hi = n // PLANE
    p, h, lo, xnb, ynb = places(n)
    pos = lax.axis_index("frame")
    lox = xnb % PLANE
    ring = [(p + n - 1) % n, (p + 1) % n]
    bs, es = (b0, b1, b2), (e0, e1, e2)

    def rows(hh, ll):
        return o_ref.at[pl.ds(pl.multiple_of((hh * PLANE + ll) * w, w), w)]

    def half(ref, d, which):
        return ref.at[pl.ds(pl.multiple_of((2 * d + which) * hs, hs), hs)]

    zpeer = [((h + j) % hi) * PLANE + lo for j in range(hi)]
    greet(zpeer[1:] + [xnb, ynb] + ring, pos)
    order = sorted(range(1, hi), key=lambda j: min(j, hi - j))
    mine = rows(h, lo)
    zc = {j: send(x_ref, mine, zs.at[j], zr.at[j], zpeer[j]) for j in order}
    xc, yc, rc, hc, fc = {}, {}, {}, {}, {}
    xc[0] = send(x_ref, mine, xs.at[0], xr.at[0], xnb)
    yc[0] = send(x_ref, mine, ys.at[0], yr.at[0], ynb)
    xc[0].start()
    yc[0].start()
    for j in reversed(order):
        zc[j].start()
    rest = [send(r_ref.at[d], t_ref.at[1 - d], qs.at[d], qr.at[d], ring[d]) for d in range(2)]
    rest[0].start()
    rest[1].start()

    def halo(c):
        for d in range(2):
            hc[c, d] = send(
                half(bs[c], d, pos), half(es[c], 1 - d, pos),
                hds.at[2 * c + d], hdr.at[2 * c + d], ring[d],
            )
            hc[c, d].start()

    def swap(c):
        for d in range(2):
            hc[c, d].wait_recv()
            part = half(es[c], 1 - d, pos)
            fc[c, d] = pltpu.make_async_remote_copy(
                src_ref=part, dst_ref=part,
                send_sem=fs.at[2 * c + d], recv_sem=fr.at[2 * c + d],
                device_id={"frame": 1 - pos}, device_id_type=MESH_ID,
            )
            fc[c, d].start()

    halo(0)
    mine[...] = x_ref[...]

    def relay(j):
        xc[j].wait_recv()
        part = rows((h + hi - j) % hi, lox)
        rc[j] = send(part, part, rs.at[j], rr.at[j], ynb)
        rc[j].start()

    last = 0
    for at, j in enumerate(order):
        zc[j].wait_recv()
        part = rows((h + hi - j) % hi, lo)
        xc[j] = send(part, part, xs.at[j], xr.at[j], xnb)
        yc[j] = send(part, part, ys.at[j], yr.at[j], ynb)
        xc[j].start()
        yc[j].start()
        if at == 1:
            halo(1)
        relay(last)
        last = j
    if len(order) < 2:
        halo(1)
    halo(2)
    relay(last)
    for c in range(3):
        swap(c)
    for j in range(hi):
        yc[j].wait_recv()
        rc[j].wait_recv()
    for d in range(2):
        rest[d].wait_recv()
        rest[d].wait_send()
    for c in range(3):
        for d in range(2):
            fc[c, d].wait_recv()
            fc[c, d].wait_send()
            hc[c, d].wait_send()
    for j in range(hi):
        if j:
            zc[j].wait_send()
        xc[j].wait_send()
        yc[j].wait_send()
        rc[j].wait_send()


def gather_all(x, bsend, rsend, n):
    w, f = x.shape
    hi = n // PLANE
    slots, kk = bsend[0].shape
    vm = pl.BlockSpec(memory_space=pltpu.VMEM)
    return pl.pallas_call(
        functools.partial(gather_kernel, n, w, slots // 4),
        out_shape=[jax.ShapeDtypeStruct((n * w, f), x.dtype)]
        + [jax.ShapeDtypeStruct((slots, kk), x.dtype)] * 3
        + [jax.ShapeDtypeStruct(rsend.shape, rsend.dtype)],
        in_specs=[vm] * 5,
        out_specs=[vm] * 5,
        scratch_shapes=[DMA((hi,))] * 8 + [DMA((6,))] * 4 + [DMA((2,))] * 2,
        compiler_params=pltpu.CompilerParams(collective_id=0, has_side_effects=True),
    )(x, *bsend, rsend)


def scatter_kernel(
    n, w, g_ref, o_ref, rl, sb, cx, cy, zb, zl, ls, lr, xs, xr, ys, yr, zs, zr
):
    hi = n // PLANE
    p, h, lo, xnb, ynb = places(n)
    lox, loy = xnb % PLANE, ynb % PLANE
    lod = PLANE - 1 - lo

    def rows(j, ll):
        hh = (h + j) % hi
        return g_ref.at[pl.ds(pl.multiple_of((hh * PLANE + ll) * w, w), w)]

    zpeer = [((h + j) % hi) * PLANE + lo for j in range(hi)]
    greet(zpeer[1:] + [xnb, ynb])
    order = sorted(range(1, hi), key=lambda j: -min(j, hi - j)) + [0]
    lc, xc, yc, zc = {}, {}, {}, {}
    for j in order:
        lc[j] = send(rows(j, lod), rl.at[j], ls.at[j], lr.at[j], xnb if j % 2 == 0 else ynb)
        lc[j].start()
    for j in order:
        if j % 2 == 0:
            xc[j] = send(rows(j, lox), cx.at[j], xs.at[j], xr.at[j], xnb)
            xc[j].start()
        else:
            yc[j] = send(rows(j, loy), cy.at[j], ys.at[j], yr.at[j], ynb)
            yc[j].start()
    for j in order:
        lc[j].wait_recv()
        own = rows(j, loy if j % 2 == 0 else lox)
        sb[j] = (own[...].astype(F32) + rl[j].astype(F32)).astype(BF)
        if j % 2 == 0:
            yc[j] = send(sb.at[j], cy.at[j], ys.at[j], yr.at[j], ynb)
            yc[j].start()
        else:
            xc[j] = send(sb.at[j], cx.at[j], xs.at[j], xr.at[j], xnb)
            xc[j].start()
    for j in order:
        xc[j].wait_recv()
        yc[j].wait_recv()
        s = rows(j, lo)[...].astype(F32) + cx[j].astype(F32) + cy[j].astype(F32)
        if j:
            zb[j] = s.astype(BF)
            zc[j] = send(zb.at[j], zl.at[j], zs.at[j], zr.at[j], zpeer[j])
            zc[j].start()
    for j in reversed(order[:-1]):
        zc[j].wait_recv()
        s = s + zl[j].astype(F32)
    o_ref[...] = s
    for j in order:
        lc[j].wait_send()
        xc[j].wait_send()
        yc[j].wait_send()
        if j:
            zc[j].wait_send()


def scatter_sum(g, n):
    f = g.shape[1]
    w = g.shape[0] // n
    hi = n // PLANE
    return pl.pallas_call(
        functools.partial(scatter_kernel, n, w),
        out_shape=jax.ShapeDtypeStruct((w, f), F32),
        in_specs=[pl.BlockSpec(memory_space=pltpu.VMEM)],
        out_specs=pl.BlockSpec(memory_space=pltpu.VMEM),
        scratch_shapes=[pltpu.VMEM((hi, w, f), BF)] * 6 + [DMA((hi,))] * 8,
        compiler_params=pltpu.CompilerParams(collective_id=1, has_side_effects=True),
    )(g)


def local(basis, latents, rest_pos, triangles, hinges, rest_sq, bend_rest, masses, send_rows):
    vs = basis.shape[1]
    kk = basis.shape[2]
    ff = latents.shape[0]
    halo = send_rows.shape[1]
    nt = triangles.shape[1]
    total = ff * lax.axis_size("frame")
    pos = lax.axis_index("frame")
    n = lax.axis_size("patch")
    ext = vs + 2 * halo
    ta, tb, tc = (hot(ext, triangles[i]) for i in range(3))
    ha, hb, hc, hd = (hot(ext, hinges[i]) for i in range(4))
    inc = jnp.concatenate([tb - ta, tc - tb, hc + hd - ha - hb], axis=1).astype(BF)
    self32 = hot(vs, send_rows.reshape(-1))
    sel = self32.astype(BF)
    rest_out = exact(rest_pos, self32)
    bsend = [mm(sel, basis[c], ((0,), (0,))).astype(BF) for c in range(3)]
    rsend = jnp.pad(rest_out.reshape(3, 2, halo).transpose(1, 0, 2), ((0, 0), (0, 5), (0, 0)))
    lat_t, *bhalo, rhalo = gather_all(latents.T, bsend, rsend, n)
    lat_o = lax.ppermute(lat_t, "frame", [(0, 1), (1, 0)])
    rest_ext = jnp.concatenate([rest_pos, rhalo[0, :3], rhalo[1, :3]], axis=1)
    rest_edge = exact(rest_ext, inc.astype(F32))
    rest_edge = rest_edge.at[:, 2 * nt :].add(-bend_rest)
    flat_basis = basis.reshape(3 * vs, kk)
    dec = mm(flat_basis, lat_t, ((1,), (0,))).astype(BF).reshape(3, vs, ff)
    own = jnp.concatenate([dec[0], dec[1], dec[2]], axis=1)
    far = [mm(bhalo[c], lat_t, ((1,), (0,))).astype(BF) for c in range(3)]
    dext = jnp.concatenate([own, jnp.concatenate(far, axis=1)], axis=0)
    edges = mm(inc, dext, ((0,), (0,)))
    e1 = [edges[:nt, c * ff : (c + 1) * ff] + rest_edge[c, :nt, None] for c in range(3)]
    e2 = [edges[nt : 2 * nt, c * ff : (c + 1) * ff] + rest_edge[c, nt : 2 * nt, None] for c in range(3)]
    hh = [edges[2 * nt :, c * ff : (c + 1) * ff] + rest_edge[c, 2 * nt :, None] for c in range(3)]
    e3 = [-(a + b) for a, b in zip(e1, e2)]
    k = 4.0 * MEMBRANE / total

    def strain(e, r):
        return k * (e[0] * e[0] + e[1] * e[1] + e[2] * e[2] - r[:, None])

    s1, s2, s3 = strain(e1, rest_sq[0]), strain(e2, rest_sq[1]), strain(e3, rest_sq[2])
    u1 = jnp.concatenate([s1 * e1[c] - s3 * e3[c] for c in range(3)], axis=1)
    u2 = jnp.concatenate([s2 * e2[c] - s3 * e3[c] for c in range(3)], axis=1)
    uh = jnp.concatenate(hh, axis=1) * (2.0 * BENDING / total)
    forces = jnp.concatenate([u1, u2, uh], axis=0).astype(BF)
    g = mm(inc, forces, ((1,), (0,)))
    gh = g[vs:].astype(BF)
    back = jnp.concatenate([shift(gh[halo:], 1), shift(gh[:halo], -1)], axis=0)
    owned = g[:vs] + mm(sel, back, ((1,), (0,)))
    owned = owned.at[:, 2 * ff :].add((GRAVITY / total) * masses[:, None])
    adj = owned.astype(BF)
    half = vs // 2
    mine = lax.dynamic_slice_in_dim(adj, pos * half, half, 0)
    other = lax.dynamic_slice_in_dim(adj, (1 - pos) * half, half, 0)
    got = lax.ppermute(other, "frame", [(0, 1), (1, 0)])

    def part(a, lat):
        a3 = jnp.concatenate([a[:, c * ff : (c + 1) * ff] for c in range(3)], axis=0)
        s = lax.optimization_barrier(mm(a3, lat, ((1,), (1,))).astype(BF))
        return s.astype(F32).reshape(3, half, kk)

    basis_grad = part(mine, lat_t) + part(got, lat_o)
    adj3 = jnp.concatenate([adj[:, c * ff : (c + 1) * ff] for c in range(3)], axis=0)
    lg_t = mm(flat_basis, adj3, ((0,), (0,))).astype(BF)
    lg = scatter_sum(lg_t, n)
    return (basis_grad, lg.T)


def solution(mesh):
    return jax.shard_map(
        local,
        mesh=mesh,
        in_specs=(
            P(None, "patch", None),
            P("frame", "patch"),
            P(None, "patch"),
            P(None, "patch"),
            P(None, "patch"),
            P(None, "patch"),
            P(None, "patch"),
            P("patch"),
            P(None, "patch"),
        ),
        out_specs=(P(None, ("patch", "frame"), None), P("frame", "patch")),
        check_vma=False,
    )
```

```python
import functools

import jax
import jax.numpy as jnp
from jax import lax
from jax.experimental import pallas as pl
from jax.experimental.pallas import tpu as pltpu
from jax.sharding import PartitionSpec as P

MEMBRANE = 5.0
BENDING = 5.0
GRAVITY = 40.0
BF = jnp.bfloat16
F32 = jnp.float32


def hot(rows, ids):
    iota = lax.broadcasted_iota(jnp.int32, (rows, ids.shape[0]), 0)
    return (iota == ids[None, :]).astype(F32)


def mm(a, b, dims):
    return lax.dot_general(a, b, (dims, ((), ())), preferred_element_type=F32)


def exact(a, b):
    return jnp.dot(a, b, precision=lax.Precision.HIGHEST, preferred_element_type=F32)


PLANE = 4
MESH_ID = pl.DeviceIdType.MESH
DMA = pltpu.SemaphoreType.DMA


def places(n):
    p = lax.axis_index("patch")
    xnb = p + 1 - 2 * (p % 2)
    ynb = p + 2 - 4 * ((p // 2) % 2)
    return p, p // PLANE, p % PLANE, xnb, ynb


def greet(peers, pos=None):
    bar = pltpu.get_barrier_semaphore()
    if pos is not None:
        pl.semaphore_signal(bar, inc=1, device_id={"frame": 1 - pos}, device_id_type=MESH_ID)
    for q in peers:
        pl.semaphore_signal(bar, inc=1, device_id={"patch": q}, device_id_type=MESH_ID)
    pl.semaphore_wait(bar, len(peers) + (pos is not None))


def send(src, dst, ss, rs, q):
    return pltpu.make_async_remote_copy(
        src_ref=src, dst_ref=dst, send_sem=ss, recv_sem=rs,
        device_id={"patch": q}, device_id_type=MESH_ID,
    )


def gather_kernel(
    n, w, hs, x_ref, b0, b1, b2, r_ref, o_ref, e0, e1, e2, t_ref,
    zs, zr, xs, xr, ys, yr, rs, rr, hds, hdr, fs, fr, qs, qr
):
    hi = n // PLANE
    p, h, lo, xnb, ynb = places(n)
    pos = lax.axis_index("frame")
    lox = xnb % PLANE
    ring = [(p + n - 1) % n, (p + 1) % n]
    bs, es = (b0, b1, b2), (e0, e1, e2)

    def rows(hh, ll):
        return o_ref.at[pl.ds(pl.multiple_of((hh * PLANE + ll) * w, w), w)]

    def half(ref, d, which):
        return ref.at[pl.ds(pl.multiple_of((2 * d + which) * hs, hs), hs)]

    zpeer = [((h + j) % hi) * PLANE + lo for j in range(hi)]
    greet(zpeer[1:] + [xnb, ynb] + ring, pos)
    order = sorted(range(1, hi), key=lambda j: min(j, hi - j))
    mine = rows(h, lo)
    zc = {j: send(x_ref, mine, zs.at[j], zr.at[j], zpeer[j]) for j in order}
    xc, yc, rc, hc, fc = {}, {}, {}, {}, {}
    xc[0] = send(x_ref, mine, xs.at[0], xr.at[0], xnb)
    yc[0] = send(x_ref, mine, ys.at[0], yr.at[0], ynb)
    xc[0].start()
    yc[0].start()
    for j in reversed(order):
        zc[j].start()
    rest = [send(r_ref.at[d], t_ref.at[1 - d], qs.at[d], qr.at[d], ring[d]) for d in range(2)]
    rest[0].start()
    rest[1].start()

    def halo(c):
        for d in range(2):
            hc[c, d] = send(
                half(bs[c], d, pos), half(es[c], 1 - d, pos),
                hds.at[2 * c + d], hdr.at[2 * c + d], ring[d],
            )
            hc[c, d].start()

    def swap(c):
        for d in range(2):
            hc[c, d].wait_recv()
            part = half(es[c], 1 - d, pos)
            fc[c, d] = pltpu.make_async_remote_copy(
                src_ref=part, dst_ref=part,
                send_sem=fs.at[2 * c + d], recv_sem=fr.at[2 * c + d],
                device_id={"frame": 1 - pos}, device_id_type=MESH_ID,
            )
            fc[c, d].start()

    halo(0)
    mine[...] = x_ref[...]

    def relay(j):
        xc[j].wait_recv()
        part = rows((h + hi - j) % hi, lox)
        rc[j] = send(part, part, rs.at[j], rr.at[j], ynb)
        rc[j].start()

    last = 0
    for at, j in enumerate(order):
        zc[j].wait_recv()
        part = rows((h + hi - j) % hi, lo)
        xc[j] = send(part, part, xs.at[j], xr.at[j], xnb)
        yc[j] = send(part, part, ys.at[j], yr.at[j], ynb)
        xc[j].start()
        yc[j].start()
        if at == 1:
            halo(1)
        relay(last)
        last = j
    if len(order) < 2:
        halo(1)
    halo(2)
    relay(last)
    for c in range(3):
        swap(c)
    for j in range(hi):
        yc[j].wait_recv()
        rc[j].wait_recv()
    for d in range(2):
        rest[d].wait_recv()
        rest[d].wait_send()
    for c in range(3):
        for d in range(2):
            fc[c, d].wait_recv()
            fc[c, d].wait_send()
            hc[c, d].wait_send()
    for j in range(hi):
        if j:
            zc[j].wait_send()
        xc[j].wait_send()
        yc[j].wait_send()
        rc[j].wait_send()


def gather_all(x, bsend, rsend, n):
    w, f = x.shape
    hi = n // PLANE
    slots, kk = bsend[0].shape
    vm = pl.BlockSpec(memory_space=pltpu.VMEM)
    return pl.pallas_call(
        functools.partial(gather_kernel, n, w, slots // 4),
        out_shape=[jax.ShapeDtypeStruct((n * w, f), x.dtype)]
        + [jax.ShapeDtypeStruct((slots, kk), x.dtype)] * 3
        + [jax.ShapeDtypeStruct(rsend.shape, rsend.dtype)],
        in_specs=[vm] * 5,
        out_specs=[vm] * 5,
        scratch_shapes=[DMA((hi,))] * 8 + [DMA((6,))] * 4 + [DMA((2,))] * 2,
        compiler_params=pltpu.CompilerParams(collective_id=0, has_side_effects=True),
    )(x, *bsend, rsend)


def tail_kernel(
    n, w, own_ref, gh_ref, sel_ref, b0, b1, b2, lt_ref, lo_ref, bg_ref, o_ref,
    bt, bk, adj, got, acc, g, rl, sb, cx, cy, zb, zl,
    ks, kr, ps, pr, ls, lr, xs, xr, ys, yr, zs, zr,
):
    hi = n // PLANE
    p, h, lo, xnb, ynb = places(n)
    pos = lax.axis_index("frame")
    lox, loy = xnb % PLANE, ynb % PLANE
    lod = PLANE - 1 - lo
    ring = [(p + n - 1) % n, (p + 1) % n]
    bs = (b0, b1, b2)
    vs, kk = b0.shape
    ff = lt_ref.shape[1]
    halo = gh_ref.shape[0] // 2
    half = vs // 2
    tile = 256

    def rows(j, ll):
        hh = (h + j) % hi
        return g.at[pl.ds(pl.multiple_of((hh * PLANE + ll) * w, w), w)]

    zpeer = [((h + j) % hi) * PLANE + lo for j in range(hi)]
    greet(zpeer[1:] + [xnb, ynb] + ring, pos)
    kc, pc = {}, []
    for c in range(3):
        for d in range(2):
            kc[c, d] = send(
                gh_ref.at[pl.ds(d * halo, halo), pl.ds(c * ff, ff)],
                bk.at[c, pl.ds((1 - d) * halo, halo)],
                ks.at[2 * c + d], kr.at[2 * c + d], ring[d],
            )
            kc[c, d].start()
    for c in range(3):
        bt[c] = bs[c][...].T
    for c in range(3):
        kc[c, 0].wait_recv()
        kc[c, 1].wait_recv()
        adj[c] = (
            own_ref[:, pl.ds(c * ff, ff)] + mm(sel_ref[...], bk[c], ((1,), (0,)))
        ).astype(BF)
        cp = pltpu.make_async_remote_copy(
            src_ref=adj.at[c, pl.ds(pl.multiple_of((1 - pos) * half, half), half)],
            dst_ref=got.at[c], send_sem=ps.at[c], recv_sem=pr.at[c],
            device_id={"frame": 1 - pos}, device_id_type=MESH_ID,
        )
        cp.start()
        pc.append(cp)
        for r in range(0, kk, tile):
            block = mm(bt[c, r : r + tile], adj[c], ((1,), (0,)))
            if c:
                block = block + acc[r : r + tile]
            if c < 2:
                acc[r : r + tile] = block
            else:
                g[r : r + tile] = block.astype(BF)

    def grad(c):
        mine = adj[c, pl.ds(pl.multiple_of(pos * half, half), half)]
        for r in range(0, kk, tile):
            one = mm(mine, lt_ref[r : r + tile], ((1,), (1,))).astype(BF).astype(F32)
            two = mm(got[c], lo_ref[r : r + tile], ((1,), (1,))).astype(BF).astype(F32)
            bg_ref[c, :, r : r + tile] = one + two

    order = sorted(range(1, hi), key=lambda j: -min(j, hi - j))
    even = [j for j in order if j % 2 == 0]
    odd = [j for j in order if j % 2]
    lc, xc, yc, zc = {}, {}, {}, {}

    def via(j):
        lc[j] = send(rows(j, lod), rl.at[j], ls.at[j], lr.at[j], ynb if j % 2 else xnb)
        lc[j].start()

    def to_x(j, src):
        xc[j] = send(src, cx.at[j], xs.at[j], xr.at[j], xnb)
        xc[j].start()

    def to_y(j, src):
        yc[j] = send(src, cy.at[j], ys.at[j], yr.at[j], ynb)
        yc[j].start()

    def summed(j):
        lc[j].wait_recv()
        own = rows(j, lox if j % 2 else loy)
        sb[j] = (own[...].astype(F32) + rl[j].astype(F32)).astype(BF)
        (to_x if j % 2 else to_y)(j, sb.at[j])

    def total(j):
        xc[j].wait_recv()
        yc[j].wait_recv()
        return rows(j, lo)[...].astype(F32) + cx[j].astype(F32) + cy[j].astype(F32)

    for j in even:
        via(j)
    for j in odd:
        via(j)
    for j in even:
        to_x(j, rows(j, lox))
    for c in range(3):
        pc[c].wait_recv()
    grad(0)
    for j in even:
        summed(j)
    for j in odd:
        to_y(j, rows(j, loy))
    for j in odd:
        summed(j)
    via(0)
    to_x(0, rows(0, lox))
    grad(1)
    for j in order:
        zb[j] = total(j).astype(BF)
        zc[j] = send(zb.at[j], zl.at[j], zs.at[j], zr.at[j], zpeer[j])
        zc[j].start()
    summed(0)
    grad(2)
    s = total(0)
    for j in reversed(order):
        zc[j].wait_recv()
        s = s + zl[j].astype(F32)
    o_ref[...] = s
    for c in range(3):
        kc[c, 0].wait_send()
        kc[c, 1].wait_send()
        pc[c].wait_send()
    for j in [0] + order:
        lc[j].wait_send()
        xc[j].wait_send()
        yc[j].wait_send()
        if j:
            zc[j].wait_send()


def tail(own, gh, sel, bases, lat_t, lat_o, n):
    kk, f = lat_t.shape
    w = kk // n
    hi = n // PLANE
    vs = own.shape[0]
    vm = pl.BlockSpec(memory_space=pltpu.VMEM)
    vmem = pltpu.VMEM
    return pl.pallas_call(
        functools.partial(tail_kernel, n, w),
        out_shape=[
            jax.ShapeDtypeStruct((3, vs // 2, kk), F32),
            jax.ShapeDtypeStruct((w, f), F32),
        ],
        in_specs=[vm] * 8,
        out_specs=[vm] * 2,
        scratch_shapes=[
            vmem((3, kk, vs), BF),
            vmem((3, gh.shape[0], f), BF),
            vmem((3, vs, f), BF),
            vmem((3, vs // 2, f), BF),
            vmem((kk, f), F32),
            vmem((kk, f), BF),
        ]
        + [vmem((hi, w, f), BF)] * 6
        + [DMA((6,))] * 2
        + [DMA((3,))] * 2
        + [DMA((hi,))] * 8,
        compiler_params=pltpu.CompilerParams(
            collective_id=1, has_side_effects=True, vmem_limit_bytes=60000 * 1024
        ),
    )(own, gh, sel, *bases, lat_t, lat_o)


def local(basis, latents, rest_pos, triangles, hinges, rest_sq, bend_rest, masses, send_rows):
    vs = basis.shape[1]
    kk = basis.shape[2]
    ff = latents.shape[0]
    halo = send_rows.shape[1]
    nt = triangles.shape[1]
    total = ff * lax.axis_size("frame")
    pos = lax.axis_index("frame")
    n = lax.axis_size("patch")
    ext = vs + 2 * halo
    ta, tb, tc = (hot(ext, triangles[i]) for i in range(3))
    ha, hb, hc, hd = (hot(ext, hinges[i]) for i in range(4))
    inc = jnp.concatenate([tb - ta, tc - tb, hc + hd - ha - hb], axis=1).astype(BF)
    self32 = hot(vs, send_rows.reshape(-1))
    sel = self32.astype(BF)
    rest_out = exact(rest_pos, self32)
    bsend = [mm(sel, basis[c], ((0,), (0,))).astype(BF) for c in range(3)]
    rsend = jnp.pad(rest_out.reshape(3, 2, halo).transpose(1, 0, 2), ((0, 0), (0, 5), (0, 0)))
    lat_t, *bhalo, rhalo = gather_all(latents.T, bsend, rsend, n)
    lat_o = lax.ppermute(lat_t, "frame", [(0, 1), (1, 0)])
    rest_ext = jnp.concatenate([rest_pos, rhalo[0, :3], rhalo[1, :3]], axis=1)
    rest_edge = exact(rest_ext, inc.astype(F32))
    rest_edge = rest_edge.at[:, 2 * nt :].add(-bend_rest)
    flat_basis = basis.reshape(3 * vs, kk)
    dec = mm(flat_basis, lat_t, ((1,), (0,))).astype(BF).reshape(3, vs, ff)
    own = jnp.concatenate([dec[0], dec[1], dec[2]], axis=1)
    far = [mm(bhalo[c], lat_t, ((1,), (0,))).astype(BF) for c in range(3)]
    dext = jnp.concatenate([own, jnp.concatenate(far, axis=1)], axis=0)
    edges = mm(inc, dext, ((0,), (0,)))
    e1 = [edges[:nt, c * ff : (c + 1) * ff] + rest_edge[c, :nt, None] for c in range(3)]
    e2 = [edges[nt : 2 * nt, c * ff : (c + 1) * ff] + rest_edge[c, nt : 2 * nt, None] for c in range(3)]
    hh = [edges[2 * nt :, c * ff : (c + 1) * ff] + rest_edge[c, 2 * nt :, None] for c in range(3)]
    e3 = [-(a + b) for a, b in zip(e1, e2)]
    k = 4.0 * MEMBRANE / total

    def strain(e, r):
        return k * (e[0] * e[0] + e[1] * e[1] + e[2] * e[2] - r[:, None])

    s1, s2, s3 = strain(e1, rest_sq[0]), strain(e2, rest_sq[1]), strain(e3, rest_sq[2])
    u1 = jnp.concatenate([s1 * e1[c] - s3 * e3[c] for c in range(3)], axis=1)
    u2 = jnp.concatenate([s2 * e2[c] - s3 * e3[c] for c in range(3)], axis=1)
    uh = jnp.concatenate(hh, axis=1) * (2.0 * BENDING / total)
    forces = jnp.concatenate([u1, u2, uh], axis=0).astype(BF)
    g = mm(inc, forces, ((1,), (0,)))
    gh = g[vs:].astype(BF)
    owned = g[:vs].at[:, 2 * ff :].add((GRAVITY / total) * masses[:, None])
    bases = [basis[c] for c in range(3)]
    basis_grad, lg = tail(owned, gh, sel, bases, lat_t, lat_o, n)
    return (basis_grad, lg.T)


def solution(mesh):
    return jax.shard_map(
        local,
        mesh=mesh,
        in_specs=(
            P(None, "patch", None),
            P("frame", "patch"),
            P(None, "patch"),
            P(None, "patch"),
            P(None, "patch"),
            P(None, "patch"),
            P(None, "patch"),
            P("patch"),
            P(None, "patch"),
        ),
        out_specs=(P(None, ("patch", "frame"), None), P("frame", "patch")),
        check_vma=False,
    )
```

```python
import functools

import jax
import jax.numpy as jnp
from jax import lax
from jax.experimental import pallas as pl
from jax.experimental.pallas import tpu as pltpu
from jax.sharding import PartitionSpec as P

MEMBRANE = 5.0
BENDING = 5.0
GRAVITY = 40.0
BF = jnp.bfloat16
F32 = jnp.float32


def hot(rows, ids):
    iota = lax.broadcasted_iota(jnp.int32, (rows, ids.shape[0]), 0)
    return (iota == ids[None, :]).astype(F32)


def mm(a, b, dims):
    return lax.dot_general(a, b, (dims, ((), ())), preferred_element_type=F32)


def exact(a, b):
    return jnp.dot(a, b, precision=lax.Precision.HIGHEST, preferred_element_type=F32)


PLANE = 4
MESH_ID = pl.DeviceIdType.MESH
DMA = pltpu.SemaphoreType.DMA


def places(n):
    p = lax.axis_index("patch")
    xnb = p + 1 - 2 * (p % 2)
    ynb = p + 2 - 4 * ((p // 2) % 2)
    return p, p // PLANE, p % PLANE, xnb, ynb


def greet(peers, pos=None):
    bar = pltpu.get_barrier_semaphore()
    if pos is not None:
        pl.semaphore_signal(bar, inc=1, device_id={"frame": 1 - pos}, device_id_type=MESH_ID)
    for q in peers:
        pl.semaphore_signal(bar, inc=1, device_id={"patch": q}, device_id_type=MESH_ID)
    pl.semaphore_wait(bar, len(peers) + (pos is not None))


def send(src, dst, ss, rs, q):
    return pltpu.make_async_remote_copy(
        src_ref=src, dst_ref=dst, send_sem=ss, recv_sem=rs,
        device_id={"patch": q}, device_id_type=MESH_ID,
    )


def gather_kernel(
    n, w, x_ref, b0, b1, b2, sel_ref, r_ref, o_ref, d_ref, t_ref, hb, he,
    zs, zr, xs, xr, ys, yr, rs, rr, hds, hdr, fs, fr, qs, qr
):
    hi = n // PLANE
    p, h, lo, xnb, ynb = places(n)
    pos = lax.axis_index("frame")
    lox, loy = xnb % PLANE, ynb % PLANE
    ring = [(p + n - 1) % n, (p + 1) % n]
    bs = (b0, b1, b2)
    vs = b0.shape[0]
    ff = x_ref.shape[1]
    hs = sel_ref.shape[1] // 4

    def rows(hh, ll):
        return o_ref.at[pl.ds(pl.multiple_of((hh * PLANE + ll) * w, w), w)]

    def half(ref, c, d, which):
        return ref.at[c, pl.ds(pl.multiple_of((2 * d + which) * hs, hs), hs)]

    zpeer = [((h + j) % hi) * PLANE + lo for j in range(hi)]
    greet(zpeer[1:] + [xnb, ynb] + ring, pos)
    order = sorted(range(1, hi), key=lambda j: min(j, hi - j))
    mine = rows(h, lo)
    zc = {j: send(x_ref, mine, zs.at[j], zr.at[j], zpeer[j]) for j in order}
    xc, yc, rc, hc, fc = {}, {}, {}, {}, {}
    xc[0] = send(x_ref, mine, xs.at[0], xr.at[0], xnb)
    yc[0] = send(x_ref, mine, ys.at[0], yr.at[0], ynb)
    xc[0].start()
    yc[0].start()
    for j in reversed(order):
        zc[j].start()
    rest = [send(r_ref.at[d], t_ref.at[1 - d], qs.at[d], qr.at[d], ring[d]) for d in range(2)]
    rest[0].start()
    rest[1].start()

    def halo(c):
        for d in range(2):
            hc[c, d] = send(
                half(hb, c, d, pos), half(he, c, 1 - d, pos),
                hds.at[2 * c + d], hdr.at[2 * c + d], ring[d],
            )
            hc[c, d].start()

    def swap(c):
        for d in range(2):
            hc[c, d].wait_recv()
            part = half(he, c, 1 - d, pos)
            fc[c, d] = pltpu.make_async_remote_copy(
                src_ref=part, dst_ref=part,
                send_sem=fs.at[2 * c + d], recv_sem=fr.at[2 * c + d],
                device_id={"frame": 1 - pos}, device_id_type=MESH_ID,
            )
            fc[c, d].start()

    def decode(c, src, at, count):
        d_ref[at : at + count, c * ff : (c + 1) * ff] = mm(
            src, o_ref[...], ((1,), (0,))
        ).astype(BF)

    def far(c):
        fc[c, 0].wait_recv()
        fc[c, 1].wait_recv()
        decode(c, he[c], vs, 4 * hs)

    for c in range(3):
        hb[c] = mm(sel_ref[...], bs[c][...], ((0,), (0,))).astype(BF)
        if c == 0:
            halo(0)
    mine[...] = x_ref[...]

    def relay(j):
        hh = (h + hi - j) % hi
        (yc if j % 2 else xc)[j].wait_recv()
        part = rows(hh, loy if j % 2 else lox)
        rc[j] = send(part, part, rs.at[j], rr.at[j], xnb if j % 2 else ynb)
        rc[j].start()

    last = 0
    for at, j in enumerate(order):
        zc[j].wait_recv()
        part = rows((h + hi - j) % hi, lo)
        xc[j] = send(part, part, xs.at[j], xr.at[j], xnb)
        yc[j] = send(part, part, ys.at[j], yr.at[j], ynb)
        xc[j].start()
        yc[j].start()
        if at == 1:
            halo(1)
        relay(last)
        last = j
    if len(order) < 2:
        halo(1)
    relay(last)
    halo(2)
    for j in range(hi):
        (xc if j % 2 else yc)[j].wait_recv()
        rc[j].wait_recv()
    swap(0)
    for c in range(3):
        decode(c, bs[c][...], 0, vs)
    swap(1)
    far(0)
    swap(2)
    far(1)
    far(2)
    for d in range(2):
        rest[d].wait_recv()
        rest[d].wait_send()
    for c in range(3):
        for d in range(2):
            fc[c, d].wait_send()
            hc[c, d].wait_send()
    for j in range(hi):
        if j:
            zc[j].wait_send()
        xc[j].wait_send()
        yc[j].wait_send()
        rc[j].wait_send()


def gather_all(x, bases, sel, rsend, n):
    w, f = x.shape
    hi = n // PLANE
    vs, kk = bases[0].shape
    slots = sel.shape[1]
    vm = pl.BlockSpec(memory_space=pltpu.VMEM)
    return pl.pallas_call(
        functools.partial(gather_kernel, n, w),
        out_shape=[
            jax.ShapeDtypeStruct((n * w, f), x.dtype),
            jax.ShapeDtypeStruct((vs + slots, 3 * f), x.dtype),
            jax.ShapeDtypeStruct(rsend.shape, rsend.dtype),
        ],
        in_specs=[vm] * 6,
        out_specs=[vm] * 3,
        scratch_shapes=[pltpu.VMEM((3, slots, kk), x.dtype)] * 2
        + [DMA((hi,))] * 8 + [DMA((6,))] * 4 + [DMA((2,))] * 2,
        compiler_params=pltpu.CompilerParams(
            collective_id=0, has_side_effects=True, vmem_limit_bytes=60000 * 1024
        ),
    )(x, *bases, sel, rsend)


def tail_kernel(
    n, w, own_ref, gh_ref, sel_ref, b0, b1, b2, lt_ref, lo_ref, bg_ref, o_ref,
    bt, bk, adj, got, acc, g, rl, sb, cx, cy, zb, zl,
    ks, kr, ps, pr, ls, lr, xs, xr, ys, yr, zs, zr,
):
    hi = n // PLANE
    p, h, lo, xnb, ynb = places(n)
    pos = lax.axis_index("frame")
    lox, loy = xnb % PLANE, ynb % PLANE
    lod = PLANE - 1 - lo
    ring = [(p + n - 1) % n, (p + 1) % n]
    bs = (b0, b1, b2)
    vs, kk = b0.shape
    ff = lt_ref.shape[1]
    halo = gh_ref.shape[0] // 2
    half = vs // 2
    tile = 256

    def rows(j, ll):
        hh = (h + j) % hi
        return g.at[pl.ds(pl.multiple_of((hh * PLANE + ll) * w, w), w)]

    zpeer = [((h + j) % hi) * PLANE + lo for j in range(hi)]
    greet(zpeer[1:] + [xnb, ynb] + ring, pos)
    kc, pc = {}, []
    for c in range(3):
        for d in range(2):
            kc[c, d] = send(
                gh_ref.at[pl.ds(d * halo, halo), pl.ds(c * ff, ff)],
                bk.at[c, pl.ds((1 - d) * halo, halo)],
                ks.at[2 * c + d], kr.at[2 * c + d], ring[d],
            )
            kc[c, d].start()
    for c in range(3):
        bt[c] = bs[c][...].T
    for c in range(3):
        kc[c, 0].wait_recv()
        kc[c, 1].wait_recv()
        adj[c] = (
            own_ref[:, pl.ds(c * ff, ff)] + mm(sel_ref[...], bk[c], ((1,), (0,)))
        ).astype(BF)
        cp = pltpu.make_async_remote_copy(
            src_ref=adj.at[c, pl.ds(pl.multiple_of((1 - pos) * half, half), half)],
            dst_ref=got.at[c], send_sem=ps.at[c], recv_sem=pr.at[c],
            device_id={"frame": 1 - pos}, device_id_type=MESH_ID,
        )
        cp.start()
        pc.append(cp)
        for r in range(0, kk, tile):
            block = mm(bt[c, r : r + tile], adj[c], ((1,), (0,)))
            if c:
                block = block + acc[r : r + tile]
            if c < 2:
                acc[r : r + tile] = block
            else:
                g[r : r + tile] = block.astype(BF)

    def grad(c):
        mine = adj[c, pl.ds(pl.multiple_of(pos * half, half), half)]
        for r in range(0, kk, tile):
            one = mm(mine, lt_ref[r : r + tile], ((1,), (1,))).astype(BF).astype(F32)
            two = mm(got[c], lo_ref[r : r + tile], ((1,), (1,))).astype(BF).astype(F32)
            bg_ref[c, :, r : r + tile] = one + two

    order = sorted(range(1, hi), key=lambda j: -min(j, hi - j))
    even = [j for j in order if j % 2 == 0]
    odd = [j for j in order if j % 2]
    lc, xc, yc, zc = {}, {}, {}, {}

    def via(j):
        lc[j] = send(rows(j, lod), rl.at[j], ls.at[j], lr.at[j], ynb if j % 2 else xnb)
        lc[j].start()

    def to_x(j, src):
        xc[j] = send(src, cx.at[j], xs.at[j], xr.at[j], xnb)
        xc[j].start()

    def to_y(j, src):
        yc[j] = send(src, cy.at[j], ys.at[j], yr.at[j], ynb)
        yc[j].start()

    def summed(j):
        lc[j].wait_recv()
        own = rows(j, lox if j % 2 else loy)
        sb[j] = (own[...].astype(F32) + rl[j].astype(F32)).astype(BF)
        (to_x if j % 2 else to_y)(j, sb.at[j])

    def total(j):
        xc[j].wait_recv()
        yc[j].wait_recv()
        return rows(j, lo)[...].astype(F32) + cx[j].astype(F32) + cy[j].astype(F32)

    for j in even:
        via(j)
    for j in odd:
        via(j)
    for j in even:
        to_x(j, rows(j, lox))
    for c in range(3):
        pc[c].wait_recv()
    grad(0)
    for j in even:
        summed(j)
    for j in odd:
        to_y(j, rows(j, loy))
    for j in odd:
        summed(j)
    via(0)
    to_x(0, rows(0, lox))
    grad(1)
    for j in order:
        zb[j] = total(j).astype(BF)
        zc[j] = send(zb.at[j], zl.at[j], zs.at[j], zr.at[j], zpeer[j])
        zc[j].start()
    summed(0)
    grad(2)
    s = total(0)
    for j in reversed(order):
        zc[j].wait_recv()
        s = s + zl[j].astype(F32)
    o_ref[...] = s
    for c in range(3):
        kc[c, 0].wait_send()
        kc[c, 1].wait_send()
        pc[c].wait_send()
    for j in [0] + order:
        lc[j].wait_send()
        xc[j].wait_send()
        yc[j].wait_send()
        if j:
            zc[j].wait_send()


def tail(own, gh, sel, bases, lat_t, lat_o, n):
    kk, f = lat_t.shape
    w = kk // n
    hi = n // PLANE
    vs = own.shape[0]
    vm = pl.BlockSpec(memory_space=pltpu.VMEM)
    vmem = pltpu.VMEM
    return pl.pallas_call(
        functools.partial(tail_kernel, n, w),
        out_shape=[
            jax.ShapeDtypeStruct((3, vs // 2, kk), F32),
            jax.ShapeDtypeStruct((w, f), F32),
        ],
        in_specs=[vm] * 8,
        out_specs=[vm] * 2,
        scratch_shapes=[
            vmem((3, kk, vs), BF),
            vmem((3, gh.shape[0], f), BF),
            vmem((3, vs, f), BF),
            vmem((3, vs // 2, f), BF),
            vmem((kk, f), F32),
            vmem((kk, f), BF),
        ]
        + [vmem((hi, w, f), BF)] * 6
        + [DMA((6,))] * 2
        + [DMA((3,))] * 2
        + [DMA((hi,))] * 8,
        compiler_params=pltpu.CompilerParams(
            collective_id=1, has_side_effects=True, vmem_limit_bytes=60000 * 1024
        ),
    )(own, gh, sel, *bases, lat_t, lat_o)


def local(basis, latents, rest_pos, triangles, hinges, rest_sq, bend_rest, masses, send_rows):
    vs = basis.shape[1]
    ff = latents.shape[0]
    halo = send_rows.shape[1]
    nt = triangles.shape[1]
    total = ff * lax.axis_size("frame")
    pos = lax.axis_index("frame")
    n = lax.axis_size("patch")
    ext = vs + 2 * halo
    ta, tb, tc = (hot(ext, triangles[i]) for i in range(3))
    ha, hb, hc, hd = (hot(ext, hinges[i]) for i in range(4))
    inc = jnp.concatenate([tb - ta, tc - tb, hc + hd - ha - hb], axis=1).astype(BF)
    self32 = hot(vs, send_rows.reshape(-1))
    sel = self32.astype(BF)
    rest_out = exact(rest_pos, self32)
    bases = [basis[c] for c in range(3)]
    rsend = jnp.pad(rest_out.reshape(3, 2, halo).transpose(1, 0, 2), ((0, 0), (0, 5), (0, 0)))
    lat_t, dext, rhalo = gather_all(latents.T, bases, sel, rsend, n)
    lat_o = lax.ppermute(lat_t, "frame", [(0, 1), (1, 0)])
    rest_ext = jnp.concatenate([rest_pos, rhalo[0, :3], rhalo[1, :3]], axis=1)
    rest_edge = exact(rest_ext, inc.astype(F32))
    rest_edge = rest_edge.at[:, 2 * nt :].add(-bend_rest)
    edges = mm(inc, dext, ((0,), (0,)))
    e1 = [edges[:nt, c * ff : (c + 1) * ff] + rest_edge[c, :nt, None] for c in range(3)]
    e2 = [edges[nt : 2 * nt, c * ff : (c + 1) * ff] + rest_edge[c, nt : 2 * nt, None] for c in range(3)]
    hh = [edges[2 * nt :, c * ff : (c + 1) * ff] + rest_edge[c, 2 * nt :, None] for c in range(3)]
    e3 = [-(a + b) for a, b in zip(e1, e2)]
    k = 4.0 * MEMBRANE / total

    def strain(e, r):
        return k * (e[0] * e[0] + e[1] * e[1] + e[2] * e[2] - r[:, None])

    s1, s2, s3 = strain(e1, rest_sq[0]), strain(e2, rest_sq[1]), strain(e3, rest_sq[2])
    u1 = jnp.concatenate([s1 * e1[c] - s3 * e3[c] for c in range(3)], axis=1)
    u2 = jnp.concatenate([s2 * e2[c] - s3 * e3[c] for c in range(3)], axis=1)
    uh = jnp.concatenate(hh, axis=1) * (2.0 * BENDING / total)
    forces = jnp.concatenate([u1, u2, uh], axis=0).astype(BF)
    g = mm(inc, forces, ((1,), (0,)))
    gh = g[vs:].astype(BF)
    owned = g[:vs].at[:, 2 * ff :].add((GRAVITY / total) * masses[:, None])
    basis_grad, lg = tail(owned, gh, sel, bases, lat_t, lat_o, n)
    return (basis_grad, lg.T)


def solution(mesh):
    return jax.shard_map(
        local,
        mesh=mesh,
        in_specs=(
            P(None, "patch", None),
            P("frame", "patch"),
            P(None, "patch"),
            P(None, "patch"),
            P(None, "patch"),
            P(None, "patch"),
            P(None, "patch"),
            P("patch"),
            P(None, "patch"),
        ),
        out_specs=(P(None, ("patch", "frame"), None), P("frame", "patch")),
        check_vma=False,
    )
```
